768 devices in a mesh: dp: 32 (over x, y_lo, core), tensor: 24 (over z, y_hi).
Axes of the slice: x: 4, y: 8 (y_hi: 2, y_lo: 4; y = y_hi * 4 + y_lo), z: 12, core: 2. Of those that a mesh axis runs over, the one named last changes fastest.
Arguments:
- normed_inputs: bfloat16 [8192, 3072], P('dp', 'tensor'), may hold values from -6 to 6
- value_cotangent: bfloat16 [8192, 3072], P('dp', 'tensor'), may hold values from -1.1953125 to 1.1953125
- hidden_cotangent: bfloat16 [8192, 12288], P('dp', 'tensor'), may hold values from -1.1953125 to 1.1953125
- value_weight: bfloat16 [3072, 3072], P(None, 'tensor'), may hold values from -0.109375 to 0.109375
- hidden_weight: bfloat16 [3072, 12288], P(None, 'tensor'), may hold values from -0.109375 to 0.109375
Outputs:
- input_gradient: bfloat16 [8192, 3072], P('dp', 'tensor')
- value_weight_gradient: bfloat16 [3072, 3072], P('dp', 'tensor')
- hidden_weight_gradient: bfloat16 [3072, 12288], P('dp', 'tensor')
The draws below stay inside these ranges and needn't reach their ends.
All inputs are finite; a program needn't handle non-finite values.
Results may differ from the reference program's by a relative error of at most 0.001.
Values may be sent and summed in bfloat16 or wider, within the bound.
No kernel may reach another device: no remote copies, remote signals or barrier semaphores. Data moves between devices by JAX's collectives and lax.ppermute only.
A program may use at most 64 MiB of HBM per device.

```python
import jax
import jax.numpy as jnp

D = 3072
FFW = 12288
VCOLS = 3072
TOKENS = 8192


def steps_of(key, dims, split, least, top_value):
    def one(position, blocks):
        steps = jax.random.uniform(jax.random.fold_in(jax.random.fold_in(key, 6), position), (blocks,), jnp.float32, least / len(split), top_value / len(split))
        return jnp.repeat(jnp.exp(steps), dims[position] // blocks).reshape((-1,) + (1,) * (len(dims) - position - 1))

    gain = one(*split[0])
    for cut in split[1:]:
        gain = gain * one(*cut)
    return gain


def normal_values(own_key, dims, spread, bound, split=(), held_as=jnp.bfloat16):
    values = spread * jax.random.normal(own_key, dims, jnp.float32)
    if split:
        values = values * steps_of(own_key, dims, split, -0.22, 0.18)
    return jnp.clip(values, -bound, bound).astype(held_as)


def setup_inputs(seed: int = 0) -> dict:
    splits = jax.random.split(jax.random.key(seed), 6)
    normed_inputs = normal_values(splits[0], (TOKENS, D), 1.0, 6.0, ((0, 32), (1, 24)))
    value_cotangent = normal_values(splits[1], (TOKENS, VCOLS), 0.2, 1.1953125, ((0, 32), (1, 24)))
    hidden_cotangent = normal_values(splits[2], (TOKENS, FFW), 0.2, 1.1953125, ((0, 32), (1, 24)))
    value_weight = normal_values(splits[3], (D, VCOLS), D ** -0.5, 0.109375, ((1, 24),))
    hidden_weight = normal_values(splits[4], (D, FFW), D ** -0.5, 0.109375, ((1, 24),))
    return {"normed_inputs": normed_inputs, "value_cotangent": value_cotangent, "hidden_cotangent": hidden_cotangent, "value_weight": value_weight, "hidden_weight": hidden_weight}


def reference(normed_inputs, value_cotangent, hidden_cotangent, value_weight, hidden_weight):
    attention_term = jnp.dot(value_cotangent, value_weight.T, preferred_element_type=jnp.float32)
    hidden_term = jnp.dot(hidden_cotangent, hidden_weight.T, preferred_element_type=jnp.float32)
    input_gradient = (attention_term + hidden_term).astype(jnp.bfloat16)
    value_weight_gradient = jnp.dot(normed_inputs.T, value_cotangent, preferred_element_type=jnp.float32).astype(jnp.bfloat16)
    hidden_weight_gradient = jnp.dot(normed_inputs.T, hidden_cotangent, preferred_element_type=jnp.float32).astype(jnp.bfloat16)
    return input_gradient, value_weight_gradient, hidden_weight_gradient
```

```python
import jax
import jax.numpy as jnp
from jax import lax
from jax.sharding import Mesh
from jax.sharding import PartitionSpec as P

DP = ("x", "ylo", "core")
TENSOR = ("z", "yhi")
NX, NY, NC, NZ, NH = 4, 4, 2, 12, 2
ROWS = 8


def shift(n, by):
    return [(i, (i + by) % n) for i in range(n)]


def body(normed_inputs, value_cotangent, hidden_cotangent, value_weight, hidden_weight):
    f32, bf16 = jnp.float32, jnp.bfloat16
    tokens, features = normed_inputs.shape
    cols = value_cotangent.shape[1] + hidden_cotangent.shape[1]
    ylo, core, yhi = lax.axis_index("ylo"), lax.axis_index("core"), lax.axis_index("yhi")

    mine = features // NY
    groups = mine // ROWS
    with jax.named_scope("swap_inputs"):
        turned = normed_inputs.T.reshape(groups, NY, ROWS, tokens).transpose(1, 0, 2, 3)
        turned = turned.reshape(NY, 1, mine, tokens)
        turned = jnp.broadcast_to(turned, (NY, NH, mine, tokens)).reshape(NY * NH, mine, tokens)
        turned = lax.all_to_all(turned, ("ylo", "yhi"), 0, 0, tiled=True)
        turned = turned.reshape(NY, NH, mine, tokens).transpose(1, 2, 0, 3)
        turned = turned.reshape(NH * mine, NY * tokens)
    with jax.named_scope("gather_inputs"):
        gathered = lax.all_gather(turned, "z", axis=0, tiled=True)

    with jax.named_scope("input_terms"):
        terms = lax.dot_general(
            value_weight, value_cotangent, (((1,), (1,)), ((), ())), preferred_element_type=f32
        ) + lax.dot_general(
            hidden_weight, hidden_cotangent, (((1,), (1,)), ((), ())), preferred_element_type=f32
        )
    with jax.named_scope("scatter_terms"):
        part = lax.psum_scatter(terms, "z", scatter_dimension=0, tiled=True)

    with jax.named_scope("gather_cotangents"):
        joined = jnp.concatenate([value_cotangent, hidden_cotangent], axis=1)
        joined = jnp.broadcast_to(joined[None], (NY, tokens, cols))
        joined = lax.all_to_all(joined, "ylo", 0, 0, tiled=True).reshape(NY * tokens, cols)

    with jax.named_scope("weights"):
        grad = lax.dot_general(
            gathered, joined, (((1,), (0,)), ((), ())), preferred_element_type=f32
        )
    with jax.named_scope("add_cores"):
        rows = grad.shape[0] // (NX * NY * NC)
        grad = grad.reshape(NX * NY, NC, rows, cols)
        keep = jnp.where(core == 0, grad[:, 0], grad[:, 1])
        send = jnp.where(core == 0, grad[:, 1], grad[:, 0])
        grad = keep + lax.ppermute(send, "core", shift(NC, 1))
    with jax.named_scope("add_x"):
        grad = grad.reshape(NX, NY * rows, cols)
        grad = lax.all_to_all(grad, "x", 0, 0, tiled=True)
        grad = jnp.sum(grad, axis=0).astype(bf16)
    with jax.named_scope("place_rows"):
        grad = lax.all_to_all(grad.reshape(NY, rows, cols), "ylo", 0, 0, tiled=True)
        grad = grad.reshape(NY, rows // ROWS, ROWS, cols).transpose(1, 0, 2, 3)
        grad = grad.reshape(NY * rows, cols)

    with jax.named_scope("add_yhi"):
        half = part.shape[0] // NH
        keep = jnp.where(yhi == 0, part[:half], part[half:])
        send = jnp.where(yhi == 0, part[half:], part[:half])
        input_gradient = (keep + lax.ppermute(send, "yhi", shift(NH, 1))).T.astype(bf16)

    split_at = value_cotangent.shape[1]
    return input_gradient, grad[:, :split_at], grad[:, split_at:]


def solution(mesh):
    fine = Mesh(mesh.devices.reshape(NX, NY, NC, NZ, NH), DP + TENSOR)
    both, columns = P(DP, TENSOR), P(None, TENSOR)
    return jax.shard_map(
        body,
        mesh=fine,
        in_specs=(both, both, both, columns, columns),
        out_specs=(both, both, both),
        check_vma=False,
    )
```

```python
import functools

import jax
import jax.numpy as jnp
from jax import lax
from jax.experimental import pallas as pl
from jax.experimental.pallas import tpu as pltpu
from jax.sharding import Mesh
from jax.sharding import PartitionSpec as P

DP = ("x", "ylo", "core")
TENSOR = ("z", "yhi")
NX, NY, NC, NZ, NH = 4, 4, 2, 12, 2
ROWS = 8


def shift(n, by):
    return [(i, (i + by) % n) for i in range(n)]


def ring(block):
    found, up, down = [(0, 0, block)], block, block
    half = block.shape[0] // 2
    for step in range(1, NZ // 2):
        up = lax.ppermute(up, "z", shift(NZ, 1))
        down = lax.ppermute(down, "z", shift(NZ, -1))
        found += [(-step, 0, up), (step, 0, down)]
    if NZ % 2 == 0:
        found.append((NZ // 2, 0, lax.ppermute(up[:half], "z", shift(NZ, 1))))
        found.append((NZ // 2, half, lax.ppermute(down[half:], "z", shift(NZ, -1))))
    else:
        found.append((-(NZ // 2), 0, lax.ppermute(up, "z", shift(NZ, 1))))
        found.append((NZ // 2, 0, lax.ppermute(down, "z", shift(NZ, -1))))
    return found


def weights_kernel(places, height, *refs):
    n = len(places)
    blocks, (joined, keep, send, left, right, sems) = refs[:n], refs[n:]
    z, core = lax.axis_index("z"), lax.axis_index("core")
    copies = [pltpu.make_async_copy(joined, right, sems.at[n])]
    for i, ((step, first, size), block) in enumerate(zip(places, blocks)):
        at = lax.rem(z + (step + NZ), NZ) * height + first
        rows = left.at[pl.ds(pl.multiple_of(at, 16), size), :]
        copies.append(pltpu.make_async_copy(block, rows, sems.at[i]))
    for copy in copies:
        copy.start()
    for copy in copies:
        copy.wait()
    chunk = keep.shape[1]
    per = keep.shape[0] // NX
    rows = per * NC * chunk
    for x in range(NX):
        out = jnp.dot(
            left[x * rows : (x + 1) * rows, :], right[...], preferred_element_type=jnp.float32
        )
        for i in range(per):
            first = out[2 * i * chunk : (2 * i + 1) * chunk]
            second = out[(2 * i + 1) * chunk : (2 * i + 2) * chunk]
            keep[x * per + i] = jnp.where(core == 0, first, second)
            send[x * per + i] = jnp.where(core == 0, second, first)


def weights(found, joined):
    height, tokens = found[0][2].shape
    places = tuple((step, first, block.shape[0]) for step, first, block in found)
    total, cols = NZ * height, joined.shape[1]
    out = jax.ShapeDtypeStruct((NX * NY, total // (NX * NY * NC), cols), jnp.float32)
    vmem, anywhere = pl.BlockSpec(memory_space=pltpu.VMEM), pl.BlockSpec(memory_space=pl.ANY)
    return pl.pallas_call(
        functools.partial(weights_kernel, places, height),
        name="weights",
        out_shape=(out, out),
        in_specs=[anywhere] * (len(found) + 1),
        out_specs=(vmem, vmem),
        scratch_shapes=[
            pltpu.VMEM((total, tokens), jnp.bfloat16),
            pltpu.VMEM((tokens, cols), jnp.bfloat16),
            pltpu.SemaphoreType.DMA((len(found) + 1,)),
        ],
        cost_estimate=pl.CostEstimate(
            flops=2 * total * tokens * cols,
            bytes_accessed=2 * tokens * (total + cols) + 4 * total * cols,
            transcendentals=0,
        ),
    )(*(block for _, _, block in found), joined)


def body(normed_inputs, value_cotangent, hidden_cotangent, value_weight, hidden_weight):
    f32, bf16 = jnp.float32, jnp.bfloat16
    tokens, features = normed_inputs.shape
    cols = value_cotangent.shape[1] + hidden_cotangent.shape[1]
    yhi = lax.axis_index("yhi")

    mine = features // NY
    groups = mine // ROWS
    with jax.named_scope("swap_inputs"):
        turned = normed_inputs.T.reshape(groups, NY, ROWS, tokens).transpose(1, 0, 2, 3)
        turned = turned.reshape(NY, 1, mine, tokens)
        turned = jnp.broadcast_to(turned, (NY, NH, mine, tokens)).reshape(NY * NH, mine, tokens)
        turned = lax.all_to_all(turned, ("ylo", "yhi"), 0, 0, tiled=True)
        turned = turned.reshape(NY, NH, mine, tokens).transpose(1, 2, 0, 3)
        turned = turned.reshape(NH * mine, NY * tokens)
    with jax.named_scope("gather_inputs"):
        found = ring(turned)

    with jax.named_scope("input_terms"):
        terms = lax.dot_general(
            value_weight, value_cotangent, (((1,), (1,)), ((), ())), preferred_element_type=f32
        ) + lax.dot_general(
            hidden_weight, hidden_cotangent, (((1,), (1,)), ((), ())), preferred_element_type=f32
        )
    with jax.named_scope("scatter_terms"):
        part = lax.psum_scatter(terms, "z", scatter_dimension=0, tiled=True)

    with jax.named_scope("gather_cotangents"):
        joined = jnp.concatenate([value_cotangent, hidden_cotangent], axis=1)
        joined = jnp.broadcast_to(joined[None], (NY, tokens, cols))
        joined = lax.all_to_all(joined, "ylo", 0, 0, tiled=True).reshape(NY * tokens, cols)

    with jax.named_scope("weights"):
        keep, send = weights(found, joined)
    with jax.named_scope("add_cores"):
        grad = keep + lax.ppermute(send, "core", shift(NC, 1))
        rows = grad.shape[1]
    with jax.named_scope("add_x"):
        grad = grad.reshape(NX, NY * rows, cols)
        grad = lax.all_to_all(grad, "x", 0, 0, tiled=True)
        grad = jnp.sum(grad, axis=0).astype(bf16)
    with jax.named_scope("place_rows"):
        grad = lax.all_to_all(grad.reshape(NY, rows, cols), "ylo", 0, 0, tiled=True)
        grad = grad.reshape(NY, rows // ROWS, ROWS, cols).transpose(1, 0, 2, 3)
        grad = grad.reshape(NY * rows, cols)

    with jax.named_scope("add_yhi"):
        half = part.shape[0] // NH
        keep = jnp.where(yhi == 0, part[:half], part[half:])
        send = jnp.where(yhi == 0, part[half:], part[:half])
        input_gradient = (keep + lax.ppermute(send, "yhi", shift(NH, 1))).T.astype(bf16)

    split_at = value_cotangent.shape[1]
    return input_gradient, grad[:, :split_at], grad[:, split_at:]


def solution(mesh):
    fine = Mesh(mesh.devices.reshape(NX, NY, NC, NZ, NH), DP + TENSOR)
    both, columns = P(DP, TENSOR), P(None, TENSOR)
    return jax.shard_map(
        body,
        mesh=fine,
        in_specs=(both, both, both, columns, columns),
        out_specs=(both, both, both),
        check_vma=False,
    )
```

```python
import functools

import jax
import jax.numpy as jnp
from jax import lax
from jax.experimental import pallas as pl
from jax.experimental.pallas import tpu as pltpu
from jax.sharding import Mesh
from jax.sharding import PartitionSpec as P

DP = ("x", "ylo", "core")
TENSOR = ("z", "yhi")
NX, NY, NC, NZ, NH = 4, 4, 2, 12, 2
ROWS = 8


def shift(n, by):
    return [(i, (i + by) % n) for i in range(n)]


def permute(block, by):
    return lax.ppermute(block, "z", shift(NZ, by))


def gather(block):
    size, half, far = block.shape[0], block.shape[0] // 2, NZ // 3
    below, above = permute(block, far), permute(block, -far)
    three = jnp.concatenate([block, below, above])
    arrays = (
        three,
        permute(three, 1),
        permute(three, -1),
        permute(jnp.concatenate([block, below[:half]]), 2),
        permute(jnp.concatenate([block, above[half:]]), -2),
    )
    places = [
        (i, j * size, start + step, 0, size)
        for i, start in enumerate((0, -1, 1))
        for j, step in enumerate((0, -far, far))
    ]
    places += [(3, 0, -2, 0, size), (4, 0, 2, 0, size)]
    places += [(3, size, -2 - far, 0, half), (4, size, 2 + far, half, size - half)]
    return arrays, tuple(places)


def weights_kernel(places, height, *refs):
    blocks, (joined, keep, send, left, right, sems) = refs[:-6], refs[-6:]
    z, core = lax.axis_index("z"), lax.axis_index("core")
    copies = [pltpu.make_async_copy(joined, right, sems.at[len(places)])]
    for i, (block, row, step, first, size) in enumerate(places):
        at = lax.rem(z + (step + NZ), NZ) * height + first
        rows = left.at[pl.ds(pl.multiple_of(at, 16), size), :]
        copies.append(pltpu.make_async_copy(blocks[block].at[pl.ds(row, size), :], rows, sems.at[i]))
    for copy in copies:
        copy.start()
    for copy in copies:
        copy.wait()
    chunk = keep.shape[1]
    per = keep.shape[0] // NX
    rows = per * NC * chunk
    for x in range(NX):
        out = jnp.dot(
            left[x * rows : (x + 1) * rows, :], right[...], preferred_element_type=jnp.float32
        )
        for i in range(per):
            first = out[2 * i * chunk : (2 * i + 1) * chunk]
            second = out[(2 * i + 1) * chunk : (2 * i + 2) * chunk]
            keep[x * per + i] = jnp.where(core == 0, first, second)
            send[x * per + i] = jnp.where(core == 0, second, first)


def weights(blocks, places, height, joined):
    tokens = joined.shape[0]
    total, cols = NZ * height, joined.shape[1]
    out = jax.ShapeDtypeStruct((NX * NY, total // (NX * NY * NC), cols), jnp.float32)
    vmem, anywhere = pl.BlockSpec(memory_space=pltpu.VMEM), pl.BlockSpec(memory_space=pl.ANY)
    return pl.pallas_call(
        functools.partial(weights_kernel, places, height),
        name="weights",
        out_shape=(out, out),
        in_specs=[anywhere] * (len(blocks) + 1),
        out_specs=(vmem, vmem),
        scratch_shapes=[
            pltpu.VMEM((total, tokens), jnp.bfloat16),
            pltpu.VMEM((tokens, cols), jnp.bfloat16),
            pltpu.SemaphoreType.DMA((len(places) + 1,)),
        ],
        cost_estimate=pl.CostEstimate(
            flops=2 * total * tokens * cols,
            bytes_accessed=2 * tokens * (total + cols) + 4 * total * cols,
            transcendentals=0,
        ),
    )(*blocks, joined)


def step(normed_inputs, value_cotangent, hidden_cotangent, value_weight, hidden_weight):
    f32, bf16 = jnp.float32, jnp.bfloat16
    tokens, features = normed_inputs.shape
    cols = value_cotangent.shape[1] + hidden_cotangent.shape[1]
    yhi = lax.axis_index("yhi")

    mine = features // NY
    groups = mine // ROWS
    turned = normed_inputs.T.reshape(groups, NY, ROWS, tokens).transpose(1, 0, 2, 3)
    turned = turned.reshape(NY, 1, mine, tokens)
    turned = jnp.broadcast_to(turned, (NY, NH, mine, tokens)).reshape(NY * NH, mine, tokens)
    turned = lax.all_to_all(turned, ("ylo", "yhi"), 0, 0, tiled=True)
    turned = turned.reshape(NY, NH, mine, tokens).transpose(1, 2, 0, 3)
    turned = turned.reshape(NH * mine, NY * tokens)
    blocks, places = gather(turned)

    terms = lax.dot_general(
        value_weight, value_cotangent, (((1,), (1,)), ((), ())), preferred_element_type=f32
    ) + lax.dot_general(
        hidden_weight, hidden_cotangent, (((1,), (1,)), ((), ())), preferred_element_type=f32
    )
    part = lax.psum_scatter(terms, "z", scatter_dimension=0, tiled=True)

    joined = jnp.concatenate([value_cotangent, hidden_cotangent], axis=1)
    joined = jnp.broadcast_to(joined[None], (NY, tokens, cols))
    joined = lax.all_to_all(joined, "ylo", 0, 0, tiled=True).reshape(NY * tokens, cols)

    keep, send = weights(blocks, places, turned.shape[0], joined)
    grad = keep + lax.ppermute(send, "core", shift(NC, 1))
    rows = grad.shape[1]
    grad = grad.reshape(NX, NY * rows, cols)
    grad = lax.all_to_all(grad, "x", 0, 0, tiled=True)
    grad = jnp.sum(grad, axis=0).astype(bf16)
    grad = lax.all_to_all(grad.reshape(NY, rows, cols), "ylo", 0, 0, tiled=True)
    grad = grad.reshape(NY, rows // ROWS, ROWS, cols).transpose(1, 0, 2, 3)
    grad = grad.reshape(NY * rows, cols)

    half = part.shape[0] // NH
    keep = jnp.where(yhi == 0, part[:half], part[half:])
    send = jnp.where(yhi == 0, part[half:], part[:half])
    input_gradient = (keep + lax.ppermute(send, "yhi", shift(NH, 1))).T.astype(bf16)

    split_at = value_cotangent.shape[1]
    return input_gradient, grad[:, :split_at], grad[:, split_at:]


def solution(mesh):
    fine = Mesh(mesh.devices.reshape(NX, NY, NC, NZ, NH), DP + TENSOR)
    both, columns = P(DP, TENSOR), P(None, TENSOR)
    return jax.shard_map(
        step,
        mesh=fine,
        in_specs=(both, both, both, columns, columns),
        out_specs=(both, both, both),
        check_vma=False,
    )
```

```python
import functools

import jax
import jax.numpy as jnp
from jax import lax
from jax.experimental import pallas as pl
from jax.experimental.pallas import tpu as pltpu
from jax.sharding import Mesh
from jax.sharding import PartitionSpec as P

DP = ("x", "ylo", "core")
TENSOR = ("z", "yhi")
NX, NY, NC, NZ, NH = 4, 4, 2, 12, 2
ROWS = 8


def shift(n, by):
    return [(i, (i + by) % n) for i in range(n)]


def permute(block, by):
    return lax.ppermute(block, "z", shift(NZ, by))


def gather(block):
    size, half, far = block.shape[0], block.shape[0] // 2, NZ // 3
    below, above = permute(block, far), permute(block, -far)
    three = jnp.concatenate([block, below, above])
    arrays = (
        three,
        permute(three, 1),
        permute(three, -1),
        permute(jnp.concatenate([block, below[:half]]), 2),
        permute(jnp.concatenate([block, above[half:]]), -2),
    )
    places = [
        (i, j * size, start + step, 0, size)
        for i, start in enumerate((0, -1, 1))
        for j, step in enumerate((0, -far, far))
    ]
    places += [(3, 0, -2, 0, size), (4, 0, 2, 0, size)]
    places += [(3, size, -2 - far, 0, half), (4, size, 2 + far, half, size - half)]
    return arrays, tuple(places)


def weights_kernel(places, height, *refs):
    blocks, (ours, theirs, out, left, right, sems) = refs[:-6], refs[-6:]
    z, core = lax.axis_index("z"), lax.axis_index("core")
    copies, tokens = [], ours.shape[0]
    for i, (part, at) in enumerate(((ours, core), (theirs, 1 - core))):
        rows = right.at[pl.ds(pl.multiple_of(at * tokens, 16), tokens), :]
        copies.append(pltpu.make_async_copy(part, rows, sems.at[i]))
    for i, (block, row, step, first, size) in enumerate(places):
        at = lax.rem(z + (step + NZ), NZ) * height + first
        rows = left.at[pl.ds(pl.multiple_of(at, 16), size), :]
        copies.append(pltpu.make_async_copy(blocks[block].at[pl.ds(row, size), :], rows, sems.at[2 + i]))
    for copy in copies:
        copy.start()
    for copy in copies:
        copy.wait()
    rows = out.shape[0] // NX
    for x in range(NX):
        at = pl.ds(x * rows, rows)
        out[at, :] = jnp.dot(left[at, :], right[...], preferred_element_type=jnp.float32)


def weights(blocks, places, height, ours, theirs):
    half, cols = ours.shape
    total, tokens = NZ * height, NC * half
    vmem, anywhere = pl.BlockSpec(memory_space=pltpu.VMEM), pl.BlockSpec(memory_space=pl.ANY)
    return pl.pallas_call(
        functools.partial(weights_kernel, places, height),
        name="weights",
        out_shape=jax.ShapeDtypeStruct((total, cols), jnp.float32),
        in_specs=[anywhere] * (len(blocks) + 2),
        out_specs=vmem,
        scratch_shapes=[
            pltpu.VMEM((total, tokens), jnp.bfloat16),
            pltpu.VMEM((tokens, cols), jnp.bfloat16),
            pltpu.SemaphoreType.DMA((len(places) + 2,)),
        ],
        cost_estimate=pl.CostEstimate(
            flops=2 * total * tokens * cols,
            bytes_accessed=2 * tokens * (total + cols) + 4 * total * cols,
            transcendentals=0,
        ),
    )(*blocks, ours, theirs)


def step(normed_inputs, value_cotangent, hidden_cotangent, value_weight, hidden_weight):
    f32, bf16 = jnp.float32, jnp.bfloat16
    tokens, features = normed_inputs.shape
    cols = value_cotangent.shape[1] + hidden_cotangent.shape[1]
    yhi = lax.axis_index("yhi")

    part_rows = ROWS // NC
    groups = features // (NY * ROWS)
    mine = groups * part_rows
    turned = normed_inputs.T.reshape(groups, NY, NC, part_rows, tokens)
    turned = turned.transpose(1, 2, 0, 3, 4).reshape(NY * NC, 1, mine, tokens)
    turned = jnp.broadcast_to(turned, (NY * NC, NH, mine, tokens))
    turned = turned.reshape(NY * NC * NH, mine, tokens)
    turned = lax.all_to_all(turned, ("ylo", "core", "yhi"), 0, 0, tiled=True)
    turned = turned.reshape(NY, NC, NH, mine, tokens).transpose(2, 3, 1, 0, 4)
    turned = turned.reshape(NH * mine, NC * NY * tokens)
    blocks, places = gather(turned)

    terms = lax.dot_general(
        value_weight, value_cotangent, (((1,), (1,)), ((), ())), preferred_element_type=f32
    ) + lax.dot_general(
        hidden_weight, hidden_cotangent, (((1,), (1,)), ((), ())), preferred_element_type=f32
    )
    part = lax.psum_scatter(terms, "z", scatter_dimension=0, tiled=True)

    joined = jnp.concatenate([value_cotangent, hidden_cotangent], axis=1)
    joined = jnp.broadcast_to(joined[None], (NY, tokens, cols))
    ours = lax.all_to_all(joined, "ylo", 0, 0, tiled=True).reshape(NY * tokens, cols)
    theirs = lax.ppermute(ours, "core", shift(NC, 1))

    grad = weights(blocks, places, turned.shape[0], ours, theirs)
    rows = grad.shape[0] // NX
    grad = lax.all_to_all(grad.reshape(NX, rows, cols), "x", 0, 0, tiled=True)
    grad = jnp.sum(grad, axis=0).astype(bf16)
    grad = grad.reshape(NY * NC, rows // (NY * NC), cols)
    grad = lax.all_to_all(grad, ("ylo", "core"), 0, 0, tiled=True)
    grad = grad.reshape(NY * NC, -1, part_rows, cols).transpose(1, 0, 2, 3)
    grad = grad.reshape(rows, cols)

    half = part.shape[0] // NH
    keep = jnp.where(yhi == 0, part[:half], part[half:])
    send = jnp.where(yhi == 0, part[half:], part[:half])
    input_gradient = (keep + lax.ppermute(send, "yhi", shift(NH, 1))).T.astype(bf16)

    split_at = value_cotangent.shape[1]
    return input_gradient, grad[:, :split_at], grad[:, split_at:]


def solution(mesh):
    fine = Mesh(mesh.devices.reshape(NX, NY, NC, NZ, NH), DP + TENSOR)
    both, columns = P(DP, TENSOR), P(None, TENSOR)
    return jax.shard_map(
        step,
        mesh=fine,
        in_specs=(both, both, both, columns, columns),
        out_specs=(both, both, both),
        check_vma=False,
    )
```

```python
import functools

import jax
import jax.numpy as jnp
from jax import lax
from jax.experimental import pallas as pl
from jax.experimental.pallas import tpu as pltpu
from jax.sharding import Mesh
from jax.sharding import PartitionSpec as P

DP = ("x", "ylo", "core")
TENSOR = ("z", "yhi")
NX, NY, NC, NZ, NH = 4, 4, 2, 12, 2
ROWS = 8


def shift(n, by):
    return [(i, (i + by) % n) for i in range(n)]


def permute(block, by):
    return lax.ppermute(block, "z", shift(NZ, by))


def gather(block):
    size, half, far = block.shape[0], block.shape[0] // 2, NZ // 3
    below, above = permute(block, far), permute(block, -far)
    three = jnp.concatenate([block, below, above])
    arrays = (
        three,
        permute(three, 1),
        permute(three, -1),
        permute(jnp.concatenate([block, below[:half]]), 2),
        permute(jnp.concatenate([block, above[half:]]), -2),
    )
    places = [
        (i, j * size, start + step, 0, size)
        for i, start in enumerate((0, -1, 1))
        for j, step in enumerate((0, -far, far))
    ]
    places += [(3, 0, -2, 0, size), (4, 0, 2, 0, size)]
    places += [(3, size, -2 - far, 0, half), (4, size, 2 + far, half, size - half)]
    return arrays, tuple(places)


def weights_kernel(places, *refs):
    blocks, (ours, theirs, out, left, right, sems) = refs[:-6], refs[-6:]
    z, core = lax.axis_index("z"), lax.axis_index("core")
    height = blocks[0].shape[1]
    for part, at in ((ours, core), (theirs, 1 - core)):
        pltpu.make_async_copy(part, right.at[:, at], sems.at[0]).start()
    for block, row, step, first, size in places:
        at = pl.multiple_of(lax.rem(z + (step + NZ), NZ) * height, 16)
        rows = left.at[pl.ds(first, size), pl.ds(at, height), :]
        pltpu.make_async_copy(blocks[block].at[pl.ds(row, size)], rows, sems.at[1]).start()
    pltpu.make_async_copy(right, right, sems.at[0]).wait()
    pltpu.make_async_copy(left, left, sems.at[1]).wait()
    rows, chunks = out.shape[0] // NX, left.shape[0]
    for x in range(NX):
        at = pl.ds(x * rows, rows)
        lines = jnp.concatenate([left[i, at, :] for i in range(chunks)], axis=-1)
        out[at, :] = jnp.dot(
            lines,
            right[...].reshape(lines.shape[-1], out.shape[1]),
            preferred_element_type=jnp.float32,
        )


def weights(blocks, places, ours, theirs):
    _, tokens, cols = ours.shape
    total = NZ * blocks[0].shape[1]
    chunks = NY * NC
    vmem, anywhere = pl.BlockSpec(memory_space=pltpu.VMEM), pl.BlockSpec(memory_space=pl.ANY)
    return pl.pallas_call(
        functools.partial(weights_kernel, places),
        name="weights",
        out_shape=jax.ShapeDtypeStruct((total, cols), jnp.float32),
        in_specs=[anywhere] * (len(blocks) + 2),
        out_specs=vmem,
        scratch_shapes=[
            pltpu.VMEM((chunks, total, tokens), jnp.bfloat16),
            pltpu.VMEM((NY, NC, tokens, cols), jnp.bfloat16),
            pltpu.SemaphoreType.DMA((2,)),
        ],
        cost_estimate=pl.CostEstimate(
            flops=2 * total * chunks * tokens * cols,
            bytes_accessed=2 * chunks * tokens * (total + cols) + 4 * total * cols,
            transcendentals=0,
        ),
    )(*blocks, ours, theirs)


def step(normed_inputs, value_cotangent, hidden_cotangent, value_weight, hidden_weight):
    f32, bf16 = jnp.float32, jnp.bfloat16
    tokens, features = normed_inputs.shape
    cols = value_cotangent.shape[1] + hidden_cotangent.shape[1]
    yhi = lax.axis_index("yhi")

    part_rows = ROWS // NC
    groups = features // (NY * ROWS)
    mine = groups * part_rows
    turned = normed_inputs.T.reshape(groups, NY, NC, part_rows, tokens)
    turned = turned.transpose(1, 2, 0, 3, 4).reshape(NY * NC, 1, mine, tokens)
    turned = jnp.broadcast_to(turned, (NY * NC, NH, mine, tokens))
    turned = turned.reshape(NY * NC * NH, mine, tokens)
    turned = lax.all_to_all(turned, ("ylo", "core", "yhi"), 0, 0, tiled=True)
    turned = turned.reshape(NY * NC, NH * mine, tokens)
    blocks, places = gather(turned)

    terms = lax.dot_general(
        value_weight, value_cotangent, (((1,), (1,)), ((), ())), preferred_element_type=f32
    ) + lax.dot_general(
        hidden_weight, hidden_cotangent, (((1,), (1,)), ((), ())), preferred_element_type=f32
    )
    part = lax.psum_scatter(terms, "z", scatter_dimension=0, tiled=True)

    joined = jnp.concatenate([value_cotangent, hidden_cotangent], axis=1)
    joined = jnp.broadcast_to(joined[None], (NY, tokens, cols))
    ours = lax.all_to_all(joined, "ylo", 0, 0, tiled=True)
    theirs = lax.ppermute(ours, "core", shift(NC, 1))

    grad = weights(blocks, places, ours, theirs)
    rows = grad.shape[0] // NX
    grad = lax.all_to_all(grad.reshape(NX, rows, cols), "x", 0, 0, tiled=True)
    grad = jnp.sum(grad, axis=0).astype(bf16)
    grad = grad.reshape(NY * NC, rows // (NY * NC), cols)
    grad = lax.all_to_all(grad, ("ylo", "core"), 0, 0, tiled=True)
    grad = grad.reshape(NY * NC, -1, part_rows, cols).transpose(1, 0, 2, 3)
    grad = grad.reshape(rows, cols)

    half = part.shape[0] // NH
    keep = jnp.where(yhi == 0, part[:half], part[half:])
    send = jnp.where(yhi == 0, part[half:], part[:half])
    input_gradient = (keep + lax.ppermute(send, "yhi", shift(NH, 1))).T.astype(bf16)

    split_at = value_cotangent.shape[1]
    return input_gradient, grad[:, :split_at], grad[:, split_at:]


def solution(mesh):
    fine = Mesh(mesh.devices.reshape(NX, NY, NC, NZ, NH), DP + TENSOR)
    both, columns = P(DP, TENSOR), P(None, TENSOR)
    return jax.shard_map(
        step,
        mesh=fine,
        in_specs=(both, both, both, columns, columns),
        out_specs=(both, both, both),
        check_vma=False,
    )
```

```python
import functools

import jax
import jax.numpy as jnp
from jax import lax
from jax.experimental import pallas as pl
from jax.experimental.pallas import tpu as pltpu
from jax.sharding import Mesh
from jax.sharding import PartitionSpec as P

DP = ("x", "ylo", "core")
TENSOR = ("z", "yhi")
NX, NY, NC, NZ, NH = 4, 4, 2, 12, 2
ROWS = 8


def shift(n, by):
    return [(i, (i + by) % n) for i in range(n)]


def permute(block, by):
    return lax.ppermute(block, "z", shift(NZ, by))


def gather(block):
    size, half, last = block.shape[0], block.shape[0] // 2, NZ // 2
    arrays, places, below, above = [block], [(0, 0, 0, 0, size)], block, block
    for step in range(1, last):
        below, above = permute(below, 1), permute(above, -1)
        for start, array in ((-step, below), (step, above)):
            places.append((len(arrays), 0, start, 0, size))
            arrays.append(array)
    below, above = permute(below[:half], 1), permute(above[half:], -1)
    places += [(len(arrays), 0, last, 0, half), (len(arrays) + 1, 0, last, half, size - half)]
    return arrays + [below, above], tuple(places)


def weights_kernel(places, *refs):
    blocks, (ours, theirs, out, left, right, sems) = refs[:-6], refs[-6:]
    z, core = lax.axis_index("z"), lax.axis_index("core")
    height = blocks[0].shape[1]
    for part, at in ((ours, core), (theirs, 1 - core)):
        pltpu.make_async_copy(part, right.at[:, at], sems.at[0]).start()
    for block, row, step, first, size in places:
        at = pl.multiple_of(lax.rem(z + (step + NZ), NZ) * height, 16)
        rows = left.at[pl.ds(first, size), pl.ds(at, height), :]
        pltpu.make_async_copy(blocks[block].at[pl.ds(row, size)], rows, sems.at[1]).start()
    pltpu.make_async_copy(right, right, sems.at[0]).wait()
    pltpu.make_async_copy(left, left, sems.at[1]).wait()
    rows, chunks = out.shape[0] // NX, left.shape[0]
    for x in range(NX):
        at = pl.ds(x * rows, rows)
        lines = jnp.concatenate([left[i, at, :] for i in range(chunks)], axis=-1)
        out[at, :] = jnp.dot(
            lines,
            right[...].reshape(lines.shape[-1], out.shape[1]),
            preferred_element_type=jnp.float32,
        )


def weights(blocks, places, ours, theirs):
    _, tokens, cols = ours.shape
    total = NZ * blocks[0].shape[1]
    chunks = NY * NC
    vmem, anywhere = pl.BlockSpec(memory_space=pltpu.VMEM), pl.BlockSpec(memory_space=pl.ANY)
    return pl.pallas_call(
        functools.partial(weights_kernel, places),
        name="weights",
        out_shape=jax.ShapeDtypeStruct((total, cols), jnp.float32),
        in_specs=[anywhere] * (len(blocks) + 2),
        out_specs=vmem,
        scratch_shapes=[
            pltpu.VMEM((chunks, total, tokens), jnp.bfloat16),
            pltpu.VMEM((NY, NC, tokens, cols), jnp.bfloat16),
            pltpu.SemaphoreType.DMA((2,)),
        ],
        cost_estimate=pl.CostEstimate(
            flops=2 * total * chunks * tokens * cols,
            bytes_accessed=2 * chunks * tokens * (total + cols) + 4 * total * cols,
            transcendentals=0,
        ),
    )(*blocks, ours, theirs)


def step(normed_inputs, value_cotangent, hidden_cotangent, value_weight, hidden_weight):
    f32, bf16 = jnp.float32, jnp.bfloat16
    tokens, features = normed_inputs.shape
    cols = value_cotangent.shape[1] + hidden_cotangent.shape[1]
    yhi = lax.axis_index("yhi")

    part_rows = ROWS // NC
    groups = features // (NY * ROWS)
    mine = groups * part_rows
    turned = normed_inputs.T.reshape(groups, NY, NC, part_rows, tokens)
    turned = turned.transpose(1, 2, 0, 3, 4).reshape(NY * NC, 1, mine, tokens)
    turned = jnp.broadcast_to(turned, (NY * NC, NH, mine, tokens))
    turned = turned.reshape(NY * NC * NH, mine, tokens)
    turned = lax.all_to_all(turned, ("ylo", "core", "yhi"), 0, 0, tiled=True)
    turned = turned.reshape(NY * NC, NH * mine, tokens)
    blocks, places = gather(turned)

    terms = lax.dot_general(
        value_weight, value_cotangent, (((1,), (1,)), ((), ())), preferred_element_type=f32
    ) + lax.dot_general(
        hidden_weight, hidden_cotangent, (((1,), (1,)), ((), ())), preferred_element_type=f32
    )
    part = lax.psum_scatter(terms, "z", scatter_dimension=0, tiled=True)

    joined = jnp.concatenate([value_cotangent, hidden_cotangent], axis=1)
    joined = jnp.broadcast_to(joined[None], (NY, tokens, cols))
    ours = lax.all_to_all(joined, "ylo", 0, 0, tiled=True)
    theirs = lax.ppermute(ours, "core", shift(NC, 1))

    grad = weights(blocks, places, ours, theirs)
    rows = grad.shape[0] // NX
    grad = lax.all_to_all(grad.reshape(NX, rows, cols), "x", 0, 0, tiled=True)
    grad = jnp.sum(grad, axis=0).astype(bf16)
    grad = grad.reshape(NY * NC, rows // (NY * NC), cols)
    grad = lax.all_to_all(grad, ("ylo", "core"), 0, 0, tiled=True)
    grad = grad.reshape(NY * NC, -1, part_rows, cols).transpose(1, 0, 2, 3)
    grad = grad.reshape(rows, cols)

    half = part.shape[0] // NH
    keep = jnp.where(yhi == 0, part[:half], part[half:])
    send = jnp.where(yhi == 0, part[half:], part[:half])
    input_gradient = (keep + lax.ppermute(send, "yhi", shift(NH, 1))).T.astype(bf16)

    split_at = value_cotangent.shape[1]
    return input_gradient, grad[:, :split_at], grad[:, split_at:]


def solution(mesh):
    fine = Mesh(mesh.devices.reshape(NX, NY, NC, NZ, NH), DP + TENSOR)
    both, columns = P(DP, TENSOR), P(None, TENSOR)
    return jax.shard_map(
        step,
        mesh=fine,
        in_specs=(both, both, both, columns, columns),
        out_specs=(both, both, both),
        check_vma=False,
    )
```
